512 devices in a mesh: region: 4 (over z_hi), dom: 128 (over x, y, z_lo, core).
Axes of the slice: x: 4, y: 4, z: 16 (z_hi: 4, z_lo: 4; z = z_hi * 4 + z_lo), core: 2. Of those that a mesh axis runs over, the one named last changes fastest.
Arguments:
- entity: float32 [400, 65536], P(None, 'dom'), may hold values from -3 to 3
- relation: float32 [400, 256], replicated, may hold values from -3.6 to 3.6
- head_index: int32 [262144], P(('region', 'dom')), may hold values from 0 to 511
- relation_index: int32 [262144], P(('region', 'dom')), may hold values from 0 to 255
- tail_index: int32 [262144], P(('region', 'dom')), may hold values from 0 to 511
- negative_index: int32 [589824], P(('region', 'dom')), may hold values from 0 to 511
- plan: int32 [1], replicated, may hold values from 1 to 127
- edge_count: int32 [512], P(('region', 'dom')), may hold values from 128 to 512, as said below
Outputs:
- entity_out: float32 [400, 65536], P(None, 'dom')
- relation_out: float32 [400, 256], replicated
The draws below stay inside these ranges and needn't reach their ends.
Inputs may be any that keep to these rules, and one draw needn't show every extreme that they name: Dom index i is matched with index i XOR plan[0], its partner partition. A device's active edges are its first edge_count slots; in every draw some device uses all 512.
All inputs are finite; a program needn't handle non-finite values.
Results may differ from the reference program's by a relative error of at most 0.0032.
The reference program's roundings to bfloat16 on the way count: a program that leaves them out, or rounds other values in their place, can miss the bound.
Values may be sent and summed in bfloat16 or wider, within the bound.
A program may use at most 64 MiB of HBM per device.

```python
import math
import jax
import jax.numpy as jnp
import numpy as np
from jax import lax

DIM = 400
RELS = 256
NEG = 1152
BLOCK = 512
EDGES_DEV = 512
ENTITIES = 65536
WORKERS = 512
EDGES = 262144
NEGS = 589824
N_DOM = 128


def draw_edge_count(key, part):
    values = jax.random.randint(key, (WORKERS,), EDGES_DEV // 4, EDGES_DEV + 1)
    chosen = jax.random.randint(jax.random.fold_in(key, 7), (), 0, WORKERS)
    return jnp.where(jnp.arange(WORKERS) == chosen, EDGES_DEV, values).astype(jnp.int32)


def with_ends(entries, key, least, largest):
    longest = entries.shape.index(max(entries.shape))
    spots = []
    for shift in (0, 1):
        where = [jax.random.randint(jax.random.fold_in(key, axis), (), 0, length) for axis, length in enumerate(entries.shape)]
        where[longest] = (where[longest] + shift) % entries.shape[longest]
        spots.append(tuple(where))
    return entries.at[spots[0]].set(least).at[spots[1]].set(largest)


def block_scale(stream_key, extent, split, smallest, top_value):
    def one(dim, shards_of):
        heights = jax.random.uniform(jax.random.fold_in(jax.random.fold_in(stream_key, 6), dim), (shards_of,), jnp.float32, smallest / len(split), top_value / len(split))
        return jnp.repeat(jnp.exp(heights), extent[dim] // shards_of).reshape((-1,) + (1,) * (len(extent) - dim - 1))

    gain = one(*split[0])
    for cut in split[1:]:
        gain = gain * one(*cut)
    return gain


def rank_bounds(count, skew):
    weights = [(1 << 20) // math.isqrt(grade ** skew) + 1 for grade in range(1, count + 1)]
    spread = 1 + sum(weights) // (1 << 30)
    return np.cumsum(np.array([max(1, weight // spread) for weight in weights]))


def skewed_ids(rng, shape, number_of, lean):
    table = rank_bounds(number_of, lean)
    ticket = jax.random.randint(jax.random.fold_in(rng, 1), shape, 0, int(table[number_of - 1]))
    standing = jnp.searchsorted(jnp.asarray(table, jnp.int32), ticket, side="right")
    return jax.random.permutation(jax.random.fold_in(rng, 2), number_of)[standing].astype(jnp.int32)


def gaussian(rng, extent, scale, most, shards=(), held_as=jnp.bfloat16):
    drawn = scale * jax.random.normal(rng, extent, jnp.float32)
    if shards:
        drawn = drawn * block_scale(rng, extent, shards, -0.22, 0.18)
    return jnp.clip(drawn, -most, most).astype(held_as)


def setup_inputs(seed: int = 0) -> dict:
    key_of = jax.random.split(jax.random.key(seed), 9)
    entity = gaussian(key_of[0], (DIM, ENTITIES), 0.5, 3.0, ((1, 128),), jnp.float32)
    relation = gaussian(key_of[1], (DIM, RELS), 0.6, 3.6, (), jnp.float32)
    head_index = with_ends(jax.random.randint(key_of[2], (EDGES,), 0, BLOCK), jax.random.fold_in(key_of[2], 1), 0, BLOCK - 1).astype(jnp.int32)
    relation_index = with_ends(skewed_ids(key_of[3], (EDGES,), RELS, 2), jax.random.fold_in(key_of[3], 3), 0, RELS - 1).astype(jnp.int32)
    tail_index = with_ends(jax.random.randint(key_of[4], (EDGES,), 0, BLOCK), jax.random.fold_in(key_of[4], 1), 0, BLOCK - 1).astype(jnp.int32)
    negative_index = with_ends(jax.random.randint(key_of[5], (NEGS,), 0, BLOCK), jax.random.fold_in(key_of[5], 1), 0, BLOCK - 1).astype(jnp.int32)
    plan = jax.random.randint(key_of[6], (1,), 1, N_DOM).astype(jnp.int32)
    edge_count = draw_edge_count(jax.random.fold_in(key_of[8], 71), 0)
    return {"entity": entity, "relation": relation, "head_index": head_index, "relation_index": relation_index, "tail_index": tail_index, "negative_index": negative_index, "plan": plan, "edge_count": edge_count}


entity_rate = 1.0
relation_rate = 0.1


def edge_terms(own_rows, partner_rows, relation, head_index, relation_index, tail_index, negative_index, used):
    highest = lax.Precision.HIGHEST
    halfway = own_rows.shape[0] // 2
    edge_slots = head_index.shape[0]
    negative_slots = negative_index.shape[0]
    active = (jnp.arange(edge_slots, dtype=jnp.int32) < used).astype(jnp.float32)
    selector = (jnp.arange(relation.shape[1], dtype=jnp.int32)[:, None] == relation_index[None, :]).astype(jnp.float32)
    rel_vectors = jnp.dot(relation, selector, precision=highest)
    head_vectors = jnp.take(own_rows, head_index, axis=1)
    head_real, head_imag = head_vectors[:halfway], head_vectors[halfway:]
    rel_real, rel_imag = rel_vectors[:halfway], rel_vectors[halfway:]
    query = jnp.concatenate([head_real * rel_real - head_imag * rel_imag, head_real * rel_imag + head_imag * rel_real], axis=0).astype(jnp.bfloat16)
    query_wide = query.astype(jnp.float32)
    tail_wide = jnp.take(partner_rows, tail_index, axis=1).astype(jnp.float32)
    negative_wide = jnp.take(partner_rows, negative_index, axis=1).astype(jnp.float32)
    positive = jnp.sum(query_wide * tail_wide, axis=0)
    scores = jnp.dot(query_wide.T, negative_wide, precision=highest)
    weights = (jax.nn.sigmoid(scores) * (active / negative_slots)[:, None]).astype(jnp.bfloat16).astype(jnp.float32)
    positive_grad = -jax.nn.sigmoid(-positive) * active
    pull = positive_grad * tail_wide + jnp.dot(negative_wide, weights.T, precision=highest)
    pull_real, pull_imag = pull[:halfway], pull[halfway:]
    head_term = jnp.concatenate([pull_real * rel_real + pull_imag * rel_imag, pull_imag * rel_real - pull_real * rel_imag], axis=0)
    rel_term = jnp.concatenate([pull_real * head_real + pull_imag * head_imag, pull_imag * head_real - pull_real * head_imag], axis=0)
    tail_term = positive_grad * query_wide
    negative_term = jnp.dot(query_wide, weights, precision=highest)
    empty = jnp.zeros(own_rows.shape, jnp.float32)
    head_grad = empty.at[:, head_index].add(head_term)
    partner_grad = empty.at[:, tail_index].add(tail_term).at[:, negative_index].add(negative_term)
    rel_grad = jnp.dot(rel_term, selector.T, precision=highest)
    return head_grad, partner_grad, rel_grad


def reference(entity, relation, head_index, relation_index, tail_index, negative_index, plan, edge_count):
    blocks = entity.reshape(DIM, N_DOM, BLOCK).transpose(1, 0, 2)
    partners = jnp.bitwise_xor(jnp.arange(N_DOM, dtype=jnp.int32), plan[0])
    head_table = head_index.reshape(WORKERS, EDGES_DEV)
    relation_table = relation_index.reshape(WORKERS, EDGES_DEV)
    tail_table = tail_index.reshape(WORKERS, EDGES_DEV)
    negative_table = negative_index.reshape(WORKERS, NEG)

    def visit(carry, worker):
        entity_grad, rel_grad = carry
        domain = worker % N_DOM
        partner = partners[domain]
        own_rows = blocks[domain]
        partner_rows = blocks[partner].astype(jnp.bfloat16)
        head_grad, partner_grad, rel_part = edge_terms(own_rows, partner_rows, relation, head_table[worker], relation_table[worker], tail_table[worker], negative_table[worker], edge_count[worker])
        entity_grad = entity_grad.at[domain].add(head_grad).at[partner].add(partner_grad)
        return (entity_grad, rel_grad + rel_part), None

    start = (jnp.zeros(blocks.shape, jnp.float32), jnp.zeros(relation.shape, jnp.float32))
    (entity_grad, rel_grad), _ = lax.scan(visit, start, jnp.arange(WORKERS, dtype=jnp.int32))
    entity_out = entity - entity_rate * entity_grad.transpose(1, 0, 2).reshape(DIM, ENTITIES)
    relation_out = relation - relation_rate * rel_grad
    return entity_out, relation_out
```

```python
import functools

import jax
import jax.numpy as jnp
from jax import lax
from jax.experimental import pallas as pl
from jax.experimental.pallas import tpu as pltpu
from jax.sharding import PartitionSpec as P

entity_rate = 1.0
relation_rate = 0.1

F32 = jnp.float32
BF16 = jnp.bfloat16
MESH = pl.DeviceIdType.MESH


def move(value, offset):
    if offset == 0:
        return value
    pairs = [(source, source ^ offset) for source in range(lax.axis_size("dom"))]
    return lax.ppermute(value, "dom", pairs)


def route(payload, pattern):
    low = [functools.partial(move, offset=digit) for digit in range(8)]
    high = [functools.partial(move, offset=digit << 3) for digit in range(16)]
    payload = lax.switch(pattern & 7, low, payload)
    return lax.switch(pattern >> 3, high, payload)


def split(value, parts):
    pieces = []
    for _ in range(parts):
        piece = value.astype(BF16)
        pieces.append(piece)
        value = value - piece.astype(F32)
    return pieces


NN = (((1,), (0,)), ((), ()))
NT = (((1,), (1,)), ((), ()))
TN = (((0,), (0,)), ((), ()))


def matmul(pieces, other, dims):
    total = None
    for piece in pieces:
        part = lax.dot_general(piece, other, dims, preferred_element_type=F32)
        total = part if total is None else total + part
    return total


def one_hot(rows, index):
    shape = (rows, index.shape[1])
    return jnp.where(lax.broadcasted_iota(jnp.int32, shape, 0) == index, 1.0, 0.0).astype(BF16)


def terms_kernel(
    count_ref, entity_ref, relation_ref, partner_ref, head_ref, rel_ref, tail_ref, neg_ref,
    head_grad_ref, partner_grad_ref, rel_grad_ref, wide,
):
    features, block = entity_ref.shape
    half = features // 2
    rels = relation_ref.shape[1]
    edges = head_ref.shape[1]
    negatives = neg_ref.shape[1]
    count = count_ref[0]
    head_pick = one_hot(block, head_ref[...])
    rel_pick = one_hot(rels, rel_ref[...])
    tail_pick = one_hot(block, tail_ref[...])
    head = matmul(split(entity_ref[...], 3), head_pick, NN)
    rel = matmul(split(relation_ref[...], 3), rel_pick, NN)
    head_real, head_imag = head[:half], head[half:]
    rel_real, rel_imag = rel[:half], rel[half:]
    wide[:half, :] = head_real * rel_real - head_imag * rel_imag
    wide[half:, :] = head_real * rel_imag + head_imag * rel_real
    query = wide[...].astype(BF16)
    query_wide = query.astype(F32)
    neg_pick = one_hot(block, neg_ref[...])
    times = lax.dot_general(
        jnp.ones((8, negatives), BF16), neg_pick, NT, preferred_element_type=F32
    )[:1]

    partner = partner_ref[...]
    tail = lax.dot_general(partner, tail_pick, NN, preferred_element_type=F32)
    active = jnp.where(lax.broadcasted_iota(jnp.int32, (1, edges), 1) < count, 1.0, 0.0)
    positive = jnp.sum(query_wide * tail, axis=0, keepdims=True)
    positive_grad = -jax.nn.sigmoid(-positive) * active
    scores = lax.dot_general(query, partner, TN, preferred_element_type=F32)
    share = jnp.where(
        lax.broadcasted_iota(jnp.int32, (edges, 1), 0) < count, 1.0 / negatives, 0.0
    )
    weights = (jax.nn.sigmoid(scores) * share).astype(BF16).astype(F32) * times
    weight_hi, weight_lo = split(weights, 2)
    pull = (
        positive_grad * tail
        + lax.dot_general(partner, weight_hi, NT, preferred_element_type=F32)
        + lax.dot_general(partner, weight_lo, NT, preferred_element_type=F32)
    )
    partner_grad = (
        lax.dot_general(query, weight_hi, NN, preferred_element_type=F32)
        + lax.dot_general(query, weight_lo, NN, preferred_element_type=F32)
        + matmul(split(positive_grad * query_wide, 2), tail_pick, NT)
    )
    partner_grad_ref[...] = partner_grad.astype(BF16)
    pull_real, pull_imag = pull[:half], pull[half:]
    wide[:half, :] = pull_real * head_real + pull_imag * head_imag
    wide[half:, :] = pull_imag * head_real - pull_real * head_imag
    rel_grad_ref[:features, :] = matmul(split(wide[...], 2), rel_pick, NT)
    rel_grad_ref[features:, :] = jnp.zeros((rel_grad_ref.shape[0] - features, rels), F32)
    wide[:half, :] = pull_real * rel_real + pull_imag * rel_imag
    wide[half:, :] = pull_imag * rel_real - pull_real * rel_imag
    head_grad_ref[...] = matmul(split(wide[...], 2), head_pick, NT)


def edge_terms(edge_count, entity, relation, partner, head, rel, tail, neg):
    features, block = entity.shape
    vmem = pl.BlockSpec(memory_space=pltpu.VMEM)
    return pl.pallas_call(
        terms_kernel,
        out_shape=(
            jax.ShapeDtypeStruct((features, block), F32),
            jax.ShapeDtypeStruct((features, block), BF16),
            jax.ShapeDtypeStruct((512, relation.shape[1]), F32),
        ),
        in_specs=[pl.BlockSpec(memory_space=pltpu.SMEM)] + [vmem] * 7,
        out_specs=(vmem, vmem, vmem),
        scratch_shapes=[pltpu.VMEM((features, head.shape[1]), F32)],
        name="edge_terms",
    )(edge_count, entity, relation, partner, head, rel, tail, neg)


def sums_kernel(
    entity_ref, relation_ref, head_ref, returned_ref, rel_ref,
    entity_out, relation_out,
    mine, sent, got, shared,
    core_got, core_sum, x_got, x_sum, y_got, lo_all, hi_all, whole,
    send_sem, recv_sem,
):
    features = relation_ref.shape[0]
    quarter = entity_ref.shape[1] // 4
    region = lax.axis_index("region")
    dom = lax.axis_index("dom")
    x = dom // 32
    y = lax.rem(dom // 8, 4)
    z = lax.rem(dom // 2, 4)
    core = lax.rem(dom, 2)

    def at(region=region, x=x, y=y, z=z, core=core):
        return (region, ((x * 4 + y) * 4 + z) * 2 + core)

    def turn(value, step):
        return lax.rem(value + step, 4)

    def peer(axis, step):
        if axis == "core":
            return at(core=1 - core)
        if axis == "x":
            return at(x=turn(x, step))
        if axis == "y":
            return at(y=turn(y, step))
        if axis == "z":
            return at(z=turn(z, step))
        return at(region=turn(region, step))

    barrier = pltpu.get_barrier_semaphore()
    peers = [peer("core", 1)] + [peer(a, s) for a in ("x", "y", "z", "r") for s in (1, 2, 3)]
    for other in peers:
        pl.semaphore_signal(barrier, inc=1, device_id=other, device_id_type=MESH)

    for q in range(4):
        columns = slice(q * quarter, (q + 1) * quarter)
        value = head_ref[:, columns] + returned_ref[:, columns].astype(F32)
        mine[q] = value
        sent[q] = value.astype(BF16)

    pl.semaphore_wait(barrier, len(peers))
    used = [0]

    def send(src, dst, device):
        slot = used[0]
        used[0] += 1
        copy = pltpu.make_async_remote_copy(
            src_ref=src,
            dst_ref=dst,
            send_sem=send_sem.at[slot],
            recv_sem=recv_sem.at[slot],
            device_id=device,
            device_id_type=MESH,
        )
        copy.start()
        return copy

    def wait(copies):
        for copy in copies:
            copy.wait()

    steps = (2, 1, 3)
    entity_copies = [
        send(sent.at[turn(region, s)], got.at[s - 1], peer("r", s)) for s in steps
    ]

    wait([send(rel_ref.at[1 - core], core_got, peer("core", 1))])
    core_sum[...] = rel_ref[core] + core_got[...]
    wait([send(core_sum.at[turn(x, s)], x_got.at[s - 1], peer("x", s)) for s in steps])
    x_sum[...] = core_sum[x] + x_got[0] + x_got[1] + x_got[2]
    wait([send(x_sum.at[turn(y, s)], y_got.at[s - 1], peer("y", s)) for s in steps])
    lo_all[z] = x_sum[y] + y_got[0] + y_got[1] + y_got[2]
    wait([send(lo_all.at[z], lo_all.at[z], peer("z", s)) for s in steps])
    hi_all[region] = lo_all[0] + lo_all[1] + lo_all[2] + lo_all[3]
    wait([send(hi_all.at[region], hi_all.at[region], peer("r", s)) for s in steps])
    whole[core, x, y] = hi_all[0] + hi_all[1] + hi_all[2] + hi_all[3]

    wait(entity_copies)
    total = mine[region] + got[0].astype(F32) + got[1].astype(F32) + got[2].astype(F32)
    shared[region] = total.astype(BF16)
    entity_copies = [send(shared.at[region], shared.at[region], peer("r", s)) for s in steps]

    wait([send(whole.at[core, x, y], whole.at[core, x, y], peer("y", s)) for s in steps])
    wait([send(whole.at[core, x], whole.at[core, x], peer("x", s)) for s in steps])
    wait([send(whole.at[core], whole.at[core], peer("core", 1))])
    for piece in range(features // 16):
        rows = slice(piece * 16, piece * 16 + 16)
        part = whole[piece // 16, piece // 4 % 4, piece % 4]
        relation_out[rows, :] = relation_ref[rows, :] - relation_rate * part

    wait(entity_copies)
    for q in range(4):
        columns = slice(q * quarter, (q + 1) * quarter)
        entity_out[:, columns] = entity_ref[:, columns] - entity_rate * shared[q].astype(F32)


def sum_all(entity, relation, head_grad, returned, rel_grad):
    features, block = entity.shape
    rels = relation.shape[1]
    quarter = block // 4
    vmem = pl.BlockSpec(memory_space=pltpu.VMEM)
    piece = (16, rels)
    copies = 26
    return pl.pallas_call(
        sums_kernel,
        out_shape=(
            jax.ShapeDtypeStruct(entity.shape, F32),
            jax.ShapeDtypeStruct(relation.shape, F32),
        ),
        in_specs=[vmem] * 5,
        out_specs=(vmem, vmem),
        scratch_shapes=[
            pltpu.VMEM((4, features, quarter), F32),
            pltpu.VMEM((4, features, quarter), BF16),
            pltpu.VMEM((3, features, quarter), BF16),
            pltpu.VMEM((4, features, quarter), BF16),
            pltpu.VMEM((4, 4) + piece, F32),
            pltpu.VMEM((4, 4) + piece, F32),
            pltpu.VMEM((3, 4) + piece, F32),
            pltpu.VMEM((4,) + piece, F32),
            pltpu.VMEM((3,) + piece, F32),
            pltpu.VMEM((4,) + piece, F32),
            pltpu.VMEM((4,) + piece, F32),
            pltpu.VMEM((2, 4, 4) + piece, F32),
            pltpu.SemaphoreType.DMA((copies,)),
            pltpu.SemaphoreType.DMA((copies,)),
        ],
        compiler_params=pltpu.CompilerParams(collective_id=0, has_side_effects=True),
        name="sum_all",
    )(entity, relation, head_grad, returned, rel_grad.reshape((2, 4, 4) + piece))


def shards(
    entity, relation, head_index, relation_index, tail_index, negative_index, plan, edge_count
):
    pattern = plan[0]
    partner = route(entity.astype(BF16), pattern)
    head_grad, partner_grad, rel_grad = edge_terms(
        edge_count,
        entity,
        relation,
        partner,
        head_index[None, :],
        relation_index[None, :],
        tail_index[None, :],
        negative_index[None, :],
    )
    returned = route(partner_grad, pattern)
    return sum_all(entity, relation, head_grad, returned, rel_grad)


def solution(mesh):
    in_specs = (
        P(None, "dom"),
        P(),
        P(("region", "dom")),
        P(("region", "dom")),
        P(("region", "dom")),
        P(("region", "dom")),
        P(),
        P(("region", "dom")),
    )
    out_specs = (P(None, "dom"), P())
    return jax.shard_map(shards, mesh=mesh, in_specs=in_specs, out_specs=out_specs, check_vma=False)
```

```python
import functools

import jax
import jax.numpy as jnp
from jax import lax
from jax.experimental import pallas as pl
from jax.experimental.pallas import tpu as pltpu
from jax.sharding import PartitionSpec as P

entity_rate = 1.0
relation_rate = 0.1

F32 = jnp.float32
BF16 = jnp.bfloat16
MESH = pl.DeviceIdType.MESH


def move(value, offset):
    if offset == 0:
        return value
    pairs = [(source, source ^ offset) for source in range(lax.axis_size("dom"))]
    return lax.ppermute(value, "dom", pairs)


def route(payload, pattern):
    count = lax.axis_size("dom")
    branches = [functools.partial(move, offset=offset) for offset in range(count)]
    return lax.switch(pattern, branches, payload)


def split(value, parts):
    pieces = []
    for _ in range(parts):
        piece = value.astype(BF16)
        pieces.append(piece)
        value = value - piece.astype(F32)
    return pieces


NN = (((1,), (0,)), ((), ()))
NT = (((1,), (1,)), ((), ()))
TN = (((0,), (0,)), ((), ()))


def matmul(pieces, other, dims):
    total = None
    for piece in pieces:
        part = lax.dot_general(piece, other, dims, preferred_element_type=F32)
        total = part if total is None else total + part
    return total


def one_hot(rows, index):
    shape = (rows, index.shape[1])
    return jnp.where(lax.broadcasted_iota(jnp.int32, shape, 0) == index, 1.0, 0.0).astype(BF16)


def terms_kernel(
    count_ref, entity_ref, relation_ref, partner_ref, head_ref, rel_ref, tail_ref, neg_ref,
    head_grad_ref, partner_grad_ref, rel_grad_ref, wide,
):
    features, block = entity_ref.shape
    half = features // 2
    rels = relation_ref.shape[1]
    edges = head_ref.shape[1]
    negatives = neg_ref.shape[1]
    count = count_ref[0]
    head_pick = one_hot(block, head_ref[...])
    rel_pick = one_hot(rels, rel_ref[...])
    tail_pick = one_hot(block, tail_ref[...])
    head = matmul(split(entity_ref[...], 3), head_pick, NN)
    rel = matmul(split(relation_ref[...], 3), rel_pick, NN)
    head_real, head_imag = head[:half], head[half:]
    rel_real, rel_imag = rel[:half], rel[half:]
    wide[:half, :] = head_real * rel_real - head_imag * rel_imag
    wide[half:, :] = head_real * rel_imag + head_imag * rel_real
    query = wide[...].astype(BF16)
    query_wide = query.astype(F32)
    neg_pick = one_hot(block, neg_ref[...])
    times = lax.dot_general(
        jnp.ones((8, negatives), BF16), neg_pick, NT, preferred_element_type=F32
    )[:1]

    partner = partner_ref[...]
    tail = lax.dot_general(partner, tail_pick, NN, preferred_element_type=F32)
    active = jnp.where(lax.broadcasted_iota(jnp.int32, (1, edges), 1) < count, 1.0, 0.0)
    positive = jnp.sum(query_wide * tail, axis=0, keepdims=True)
    positive_grad = -jax.nn.sigmoid(-positive) * active
    scores = lax.dot_general(query, partner, TN, preferred_element_type=F32)
    share = jnp.where(
        lax.broadcasted_iota(jnp.int32, (edges, 1), 0) < count, 1.0 / negatives, 0.0
    )
    weights = (jax.nn.sigmoid(scores) * share).astype(BF16).astype(F32) * times
    weight_hi, weight_lo = split(weights, 2)
    pull = (
        positive_grad * tail
        + lax.dot_general(partner, weight_hi, NT, preferred_element_type=F32)
        + lax.dot_general(partner, weight_lo, NT, preferred_element_type=F32)
    )
    partner_grad = (
        lax.dot_general(query, weight_hi, NN, preferred_element_type=F32)
        + lax.dot_general(query, weight_lo, NN, preferred_element_type=F32)
        + matmul(split(positive_grad * query_wide, 2), tail_pick, NT)
    )
    partner_grad_ref[...] = partner_grad.astype(BF16)
    pull_real, pull_imag = pull[:half], pull[half:]
    wide[:half, :] = pull_real * head_real + pull_imag * head_imag
    wide[half:, :] = pull_imag * head_real - pull_real * head_imag
    rel_grad_ref[:features, :] = matmul(split(wide[...], 2), rel_pick, NT)
    rel_grad_ref[features:, :] = jnp.zeros((rel_grad_ref.shape[0] - features, rels), F32)
    wide[:half, :] = pull_real * rel_real + pull_imag * rel_imag
    wide[half:, :] = pull_imag * rel_real - pull_real * rel_imag
    head_grad_ref[...] = matmul(split(wide[...], 2), head_pick, NT)


def edge_terms(edge_count, entity, relation, partner, head, rel, tail, neg):
    features, block = entity.shape
    vmem = pl.BlockSpec(memory_space=pltpu.VMEM)
    return pl.pallas_call(
        terms_kernel,
        out_shape=(
            jax.ShapeDtypeStruct((features, block), F32),
            jax.ShapeDtypeStruct((features, block), BF16),
            jax.ShapeDtypeStruct((512, relation.shape[1]), F32),
        ),
        in_specs=[pl.BlockSpec(memory_space=pltpu.SMEM)] + [vmem] * 7,
        out_specs=(vmem, vmem, vmem),
        scratch_shapes=[pltpu.VMEM((features, head.shape[1]), F32)],
        name="edge_terms",
    )(edge_count, entity, relation, partner, head, rel, tail, neg)


def sums_kernel(
    head_ref, returned_ref, rel_ref,
    entity_grad, relation_grad,
    mine, sent, got, shared,
    core_got, core_sum, x_got, x_sum, y_got, lo_all, hi_all, whole,
    send_sem, recv_sem,
):
    features, block = head_ref.shape
    quarter = block // 4
    region = lax.axis_index("region")
    dom = lax.axis_index("dom")
    x = dom // 32
    y = lax.rem(dom // 8, 4)
    z = lax.rem(dom // 2, 4)
    core = lax.rem(dom, 2)

    def at(region=region, x=x, y=y, z=z, core=core):
        return (region, ((x * 4 + y) * 4 + z) * 2 + core)

    def turn(value, step):
        return lax.rem(value + step, 4)

    def peer(axis, step):
        if axis == "core":
            return at(core=1 - core)
        if axis == "x":
            return at(x=turn(x, step))
        if axis == "y":
            return at(y=turn(y, step))
        if axis == "z":
            return at(z=turn(z, step))
        return at(region=turn(region, step))

    barrier = pltpu.get_barrier_semaphore()
    peers = [peer("core", 1)] + [peer(a, s) for a in ("x", "y", "z", "r") for s in (1, 2, 3)]
    for other in peers:
        pl.semaphore_signal(barrier, inc=1, device_id=other, device_id_type=MESH)

    for q in range(4):
        columns = slice(q * quarter, (q + 1) * quarter)
        value = head_ref[:, columns] + returned_ref[:, columns].astype(F32)
        mine[q] = value
        sent[q] = value.astype(BF16)

    pl.semaphore_wait(barrier, len(peers))
    used = [0]

    def send(src, dst, device):
        slot = used[0]
        used[0] += 1
        copy = pltpu.make_async_remote_copy(
            src_ref=src,
            dst_ref=dst,
            send_sem=send_sem.at[slot],
            recv_sem=recv_sem.at[slot],
            device_id=device,
            device_id_type=MESH,
        )
        copy.start()
        return copy

    def wait(copies):
        for copy in copies:
            copy.wait()

    steps = (2, 1, 3)
    entity_copies = [
        send(sent.at[turn(region, s)], got.at[s - 1], peer("r", s)) for s in steps
    ]

    wait([send(rel_ref.at[1 - core], core_got, peer("core", 1))])
    core_sum[...] = rel_ref[core] + core_got[...]
    wait([send(core_sum.at[turn(x, s)], x_got.at[s - 1], peer("x", s)) for s in steps])
    x_sum[...] = core_sum[x] + x_got[0] + x_got[1] + x_got[2]
    wait([send(x_sum.at[turn(y, s)], y_got.at[s - 1], peer("y", s)) for s in steps])
    lo_all[z] = x_sum[y] + y_got[0] + y_got[1] + y_got[2]
    lo_copies = [send(lo_all.at[z], lo_all.at[z], peer("z", s)) for s in steps]

    wait(entity_copies)
    total = mine[region] + got[0].astype(F32) + got[1].astype(F32) + got[2].astype(F32)
    shared[region] = total.astype(BF16)
    wait(lo_copies)
    hi_all[region] = lo_all[0] + lo_all[1] + lo_all[2] + lo_all[3]
    hi_copies = [send(hi_all.at[region], hi_all.at[region], peer("r", s)) for s in steps]
    entity_copies = [send(shared.at[region], shared.at[region], peer("r", s)) for s in steps]

    wait(hi_copies)
    whole[core, x, y] = hi_all[0] + hi_all[1] + hi_all[2] + hi_all[3]
    wait([send(whole.at[core, x, y], whole.at[core, x, y], peer("y", s)) for s in steps])
    wait([send(whole.at[core, x], whole.at[core, x], peer("x", s)) for s in steps])
    wait([send(whole.at[core], whole.at[core], peer("core", 1))])
    for piece in range(features // 16):
        part = whole[piece // 16, piece // 4 % 4, piece % 4]
        relation_grad[piece * 16 : piece * 16 + 16, :] = part

    wait(entity_copies)
    for q in range(4):
        entity_grad[:, q * quarter : (q + 1) * quarter] = shared[q]


def sum_all(head_grad, returned, rel_grad):
    features, block = head_grad.shape
    rels = rel_grad.shape[1]
    quarter = block // 4
    vmem = pl.BlockSpec(memory_space=pltpu.VMEM)
    piece = (16, rels)
    copies = 26
    return pl.pallas_call(
        sums_kernel,
        out_shape=(
            jax.ShapeDtypeStruct((features, block), BF16),
            jax.ShapeDtypeStruct((features, rels), F32),
        ),
        in_specs=[vmem] * 3,
        out_specs=(vmem, vmem),
        scratch_shapes=[
            pltpu.VMEM((4, features, quarter), F32),
            pltpu.VMEM((4, features, quarter), BF16),
            pltpu.VMEM((3, features, quarter), BF16),
            pltpu.VMEM((4, features, quarter), BF16),
            pltpu.VMEM((4, 4) + piece, F32),
            pltpu.VMEM((4, 4) + piece, F32),
            pltpu.VMEM((3, 4) + piece, F32),
            pltpu.VMEM((4,) + piece, F32),
            pltpu.VMEM((3,) + piece, F32),
            pltpu.VMEM((4,) + piece, F32),
            pltpu.VMEM((4,) + piece, F32),
            pltpu.VMEM((2, 4, 4) + piece, F32),
            pltpu.SemaphoreType.DMA((copies,)),
            pltpu.SemaphoreType.DMA((copies,)),
        ],
        compiler_params=pltpu.CompilerParams(collective_id=0, has_side_effects=True),
        name="sum_all",
    )(head_grad, returned, rel_grad.reshape((2, 4, 4) + piece))


def shards(
    entity, relation, head_index, relation_index, tail_index, negative_index, plan, edge_count
):
    pattern = plan[0]
    partner = route(entity.astype(BF16), pattern)
    head_grad, partner_grad, rel_grad = edge_terms(
        edge_count,
        entity,
        relation,
        partner,
        head_index[None, :],
        relation_index[None, :],
        tail_index[None, :],
        negative_index[None, :],
    )
    returned = route(partner_grad, pattern)
    entity_grad, relation_grad = sum_all(head_grad, returned, rel_grad)
    return entity - entity_rate * entity_grad.astype(F32), relation - relation_rate * relation_grad


def solution(mesh):
    in_specs = (
        P(None, "dom"),
        P(),
        P(("region", "dom")),
        P(("region", "dom")),
        P(("region", "dom")),
        P(("region", "dom")),
        P(),
        P(("region", "dom")),
    )
    out_specs = (P(None, "dom"), P())
    return jax.shard_map(shards, mesh=mesh, in_specs=in_specs, out_specs=out_specs, check_vma=False)
```

```python
import functools

import jax
import jax.numpy as jnp
from jax import lax
from jax.experimental import pallas as pl
from jax.experimental.pallas import tpu as pltpu
from jax.sharding import PartitionSpec as P

entity_rate = 1.0
relation_rate = 0.1

F32 = jnp.float32
BF16 = jnp.bfloat16
MESH = pl.DeviceIdType.MESH


def move(value, offset):
    if offset == 0:
        return value
    pairs = [(source, source ^ offset) for source in range(lax.axis_size("dom"))]
    return lax.ppermute(value, "dom", pairs)


def route(payload, pattern):
    low = [functools.partial(move, offset=digit) for digit in range(8)]
    high = [functools.partial(move, offset=digit << 3) for digit in range(16)]
    payload = lax.switch(pattern & 7, low, payload)
    return lax.switch(pattern >> 3, high, payload)


def split(value, parts):
    pieces = []
    for _ in range(parts):
        piece = value.astype(BF16)
        pieces.append(piece)
        value = value - piece.astype(F32)
    return pieces


NN = (((1,), (0,)), ((), ()))
NT = (((1,), (1,)), ((), ()))
TN = (((0,), (0,)), ((), ()))


def matmul(pieces, other, dims):
    total = None
    for piece in pieces:
        part = lax.dot_general(piece, other, dims, preferred_element_type=F32)
        total = part if total is None else total + part
    return total


def one_hot(rows, index):
    shape = (rows, index.shape[1])
    return jnp.where(lax.broadcasted_iota(jnp.int32, shape, 0) == index, 1.0, 0.0).astype(BF16)


def terms_kernel(
    count_ref, entity_ref, relation_ref, partner_ref, head_ref, rel_ref, tail_ref, neg_ref,
    head_grad_ref, partner_grad_ref, rel_grad_ref, wide,
):
    features, block = entity_ref.shape
    half = features // 2
    rels = relation_ref.shape[1]
    edges = head_ref.shape[1]
    negatives = neg_ref.shape[1]
    count = count_ref[0]
    head_pick = one_hot(block, head_ref[...])
    rel_pick = one_hot(rels, rel_ref[...])
    tail_pick = one_hot(block, tail_ref[...])
    head = matmul(split(entity_ref[...], 3), head_pick, NN)
    rel = matmul(split(relation_ref[...], 3), rel_pick, NN)
    head_real, head_imag = head[:half], head[half:]
    rel_real, rel_imag = rel[:half], rel[half:]
    wide[:half, :] = head_real * rel_real - head_imag * rel_imag
    wide[half:, :] = head_real * rel_imag + head_imag * rel_real
    query = wide[...].astype(BF16)
    query_wide = query.astype(F32)
    neg_pick = one_hot(block, neg_ref[...])
    times = lax.dot_general(
        jnp.ones((8, negatives), BF16), neg_pick, NT, preferred_element_type=F32
    )[:1]

    partner = partner_ref[...]
    tail = lax.dot_general(partner, tail_pick, NN, preferred_element_type=F32)
    active = jnp.where(lax.broadcasted_iota(jnp.int32, (1, edges), 1) < count, 1.0, 0.0)
    positive = jnp.sum(query_wide * tail, axis=0, keepdims=True)
    positive_grad = -jax.nn.sigmoid(-positive) * active
    scores = lax.dot_general(query, partner, TN, preferred_element_type=F32)
    share = jnp.where(
        lax.broadcasted_iota(jnp.int32, (edges, 1), 0) < count, 1.0 / negatives, 0.0
    )
    weights = (jax.nn.sigmoid(scores) * share).astype(BF16).astype(F32) * times
    weight_hi, weight_lo = split(weights, 2)
    pull = (
        positive_grad * tail
        + lax.dot_general(partner, weight_hi, NT, preferred_element_type=F32)
        + lax.dot_general(partner, weight_lo, NT, preferred_element_type=F32)
    )
    partner_grad = (
        lax.dot_general(query, weight_hi, NN, preferred_element_type=F32)
        + lax.dot_general(query, weight_lo, NN, preferred_element_type=F32)
        + matmul(split(positive_grad * query_wide, 2), tail_pick, NT)
    )
    partner_grad_ref[...] = partner_grad.astype(BF16)
    pull_real, pull_imag = pull[:half], pull[half:]
    wide[:half, :] = pull_real * head_real + pull_imag * head_imag
    wide[half:, :] = pull_imag * head_real - pull_real * head_imag
    rel_grad_ref[:features, :] = matmul(split(wide[...], 2), rel_pick, NT)
    rel_grad_ref[features:, :] = jnp.zeros((rel_grad_ref.shape[0] - features, rels), F32)
    wide[:half, :] = pull_real * rel_real + pull_imag * rel_imag
    wide[half:, :] = pull_imag * rel_real - pull_real * rel_imag
    head_grad_ref[...] = matmul(split(wide[...], 2), head_pick, NT)


def edge_terms(edge_count, entity, relation, partner, head, rel, tail, neg):
    features, block = entity.shape
    vmem = pl.BlockSpec(memory_space=pltpu.VMEM)
    return pl.pallas_call(
        terms_kernel,
        out_shape=(
            jax.ShapeDtypeStruct((features, block), F32),
            jax.ShapeDtypeStruct((features, block), BF16),
            jax.ShapeDtypeStruct((512, relation.shape[1]), F32),
        ),
        in_specs=[pl.BlockSpec(memory_space=pltpu.SMEM)] + [vmem] * 7,
        out_specs=(vmem, vmem, vmem),
        scratch_shapes=[pltpu.VMEM((features, head.shape[1]), F32)],
        name="edge_terms",
    )(edge_count, entity, relation, partner, head, rel, tail, neg)


def sums_kernel(
    head_ref, returned_ref, rel_ref,
    entity_grad, relation_grad,
    mine, sent, far_up, far_down, both_up, both_down, got, shared,
    core_got, core_sum, x_got, x_sum, y_got, lo_all, hi_all, whole,
    send_sem, recv_sem,
):
    features, block = head_ref.shape
    quarter = block // 4
    region = lax.axis_index("region")
    dom = lax.axis_index("dom")
    x = dom // 32
    y = lax.rem(dom // 8, 4)
    z = lax.rem(dom // 2, 4)
    core = lax.rem(dom, 2)

    def at(region=region, x=x, y=y, z=z, core=core):
        return (region, ((x * 4 + y) * 4 + z) * 2 + core)

    def turn(value, step):
        return lax.rem(value + step, 4)

    def peer(axis, step):
        if axis == "core":
            return at(core=1 - core)
        if axis == "x":
            return at(x=turn(x, step))
        if axis == "y":
            return at(y=turn(y, step))
        if axis == "z":
            return at(z=turn(z, step))
        return at(region=turn(region, step))

    barrier = pltpu.get_barrier_semaphore()
    peers = [peer("core", 1)] + [peer(a, s) for a in ("x", "y", "z", "r") for s in (1, 2, 3)]
    for other in peers:
        pl.semaphore_signal(barrier, inc=1, device_id=other, device_id_type=MESH)

    for q in range(4):
        columns = slice(q * quarter, (q + 1) * quarter)
        value = head_ref[:, columns] + returned_ref[:, columns].astype(F32)
        mine[q] = value
        sent[q] = value.astype(BF16)

    pl.semaphore_wait(barrier, len(peers))
    used = [0]

    def send(src, dst, device):
        slot = used[0]
        used[0] += 1
        copy = pltpu.make_async_remote_copy(
            src_ref=src,
            dst_ref=dst,
            send_sem=send_sem.at[slot],
            recv_sem=recv_sem.at[slot],
            device_id=device,
            device_id_type=MESH,
        )
        copy.start()
        return copy

    def wait(copies):
        for copy in copies:
            copy.wait()

    steps = (2, 1, 3)
    up, down, far = turn(region, 1), turn(region, 3), turn(region, 2)
    above, below = peer("r", 1), peer("r", 3)
    cut = far_up.shape[0]
    top, low = pl.ds(0, cut), pl.ds(cut, features - cut)

    far_copies = [
        send(sent.at[far, top], far_up, above),
        send(sent.at[far, low], far_down, below),
    ]
    near_copies = [
        send(sent.at[up, low], got.at[0, low], above),
        send(sent.at[down, top], got.at[1, top], below),
    ]

    wait([send(rel_ref.at[1 - core], core_got, peer("core", 1))])
    core_sum[...] = rel_ref[core] + core_got[...]
    wait([send(core_sum.at[turn(x, s)], x_got.at[s - 1], peer("x", s)) for s in steps])
    x_sum[...] = core_sum[x] + x_got[0] + x_got[1] + x_got[2]
    y_copies = [send(x_sum.at[turn(y, s)], y_got.at[s - 1], peer("y", s)) for s in steps]

    wait(far_copies)
    both_up[...] = (mine[up, :cut] + far_up[...].astype(F32)).astype(BF16)
    both_down[...] = (mine[down, cut:] + far_down[...].astype(F32)).astype(BF16)
    near_copies += [
        send(both_up, got.at[0, top], above),
        send(both_down, got.at[1, low], below),
    ]

    wait(y_copies)
    lo_all[z] = x_sum[y] + y_got[0] + y_got[1] + y_got[2]
    wait([send(lo_all.at[z], lo_all.at[z], peer("z", s)) for s in steps])
    hi_all[region] = lo_all[0] + lo_all[1] + lo_all[2] + lo_all[3]
    hi_copies = [send(hi_all.at[region], hi_all.at[region], peer("r", s)) for s in steps]

    wait(near_copies)
    total = mine[region] + got[0].astype(F32) + got[1].astype(F32)
    shared[region] = total.astype(BF16)
    relayed = [
        send(shared.at[region, top], shared.at[region, top], above),
        send(shared.at[region, low], shared.at[region, low], below),
    ]
    last_copies = [
        send(shared.at[region, low], shared.at[region, low], above),
        send(shared.at[region, top], shared.at[region, top], below),
    ]

    wait(hi_copies)
    whole[core, x, y] = hi_all[0] + hi_all[1] + hi_all[2] + hi_all[3]
    y_copies = [send(whole.at[core, x, y], whole.at[core, x, y], peer("y", s)) for s in steps]
    wait(relayed)
    last_copies += [
        send(shared.at[down, top], shared.at[down, top], above),
        send(shared.at[up, low], shared.at[up, low], below),
    ]
    wait(y_copies)
    wait([send(whole.at[core, x], whole.at[core, x], peer("x", s)) for s in steps])
    wait([send(whole.at[core], whole.at[core], peer("core", 1))])
    for piece in range(features // 16):
        part = whole[piece // 16, piece // 4 % 4, piece % 4]
        relation_grad[piece * 16 : piece * 16 + 16, :] = part

    wait(last_copies)
    for q in range(4):
        entity_grad[:, q * quarter : (q + 1) * quarter] = shared[q]


def sum_all(head_grad, returned, rel_grad):
    features, block = head_grad.shape
    rels = rel_grad.shape[1]
    quarter = block // 4
    vmem = pl.BlockSpec(memory_space=pltpu.VMEM)
    piece = (16, rels)
    copies = 32
    cut = (features // 2 + 15) // 16 * 16
    return pl.pallas_call(
        sums_kernel,
        out_shape=(
            jax.ShapeDtypeStruct((features, block), BF16),
            jax.ShapeDtypeStruct((features, rels), F32),
        ),
        in_specs=[vmem] * 3,
        out_specs=(vmem, vmem),
        scratch_shapes=[
            pltpu.VMEM((4, features, quarter), F32),
            pltpu.VMEM((4, features, quarter), BF16),
            pltpu.VMEM((cut, quarter), BF16),
            pltpu.VMEM((features - cut, quarter), BF16),
            pltpu.VMEM((cut, quarter), BF16),
            pltpu.VMEM((features - cut, quarter), BF16),
            pltpu.VMEM((2, features, quarter), BF16),
            pltpu.VMEM((4, features, quarter), BF16),
            pltpu.VMEM((4, 4) + piece, F32),
            pltpu.VMEM((4, 4) + piece, F32),
            pltpu.VMEM((3, 4) + piece, F32),
            pltpu.VMEM((4,) + piece, F32),
            pltpu.VMEM((3,) + piece, F32),
            pltpu.VMEM((4,) + piece, F32),
            pltpu.VMEM((4,) + piece, F32),
            pltpu.VMEM((2, 4, 4) + piece, F32),
            pltpu.SemaphoreType.DMA((copies,)),
            pltpu.SemaphoreType.DMA((copies,)),
        ],
        compiler_params=pltpu.CompilerParams(collective_id=0, has_side_effects=True),
        name="sum_all",
    )(head_grad, returned, rel_grad.reshape((2, 4, 4) + piece))


def shards(
    entity, relation, head_index, relation_index, tail_index, negative_index, plan, edge_count
):
    pattern = plan[0]
    partner = route(entity.astype(BF16), pattern)
    head_grad, partner_grad, rel_grad = edge_terms(
        edge_count,
        entity,
        relation,
        partner,
        head_index[None, :],
        relation_index[None, :],
        tail_index[None, :],
        negative_index[None, :],
    )
    returned = route(partner_grad, pattern)
    entity_grad, relation_grad = sum_all(head_grad, returned, rel_grad)
    return entity - entity_rate * entity_grad.astype(F32), relation - relation_rate * relation_grad


def solution(mesh):
    in_specs = (
        P(None, "dom"),
        P(),
        P(("region", "dom")),
        P(("region", "dom")),
        P(("region", "dom")),
        P(("region", "dom")),
        P(),
        P(("region", "dom")),
    )
    out_specs = (P(None, "dom"), P())
    return jax.shard_map(shards, mesh=mesh, in_specs=in_specs, out_specs=out_specs, check_vma=False)
```

```python
import functools

import jax
import jax.numpy as jnp
from jax import lax
from jax.experimental import pallas as pl
from jax.experimental.pallas import tpu as pltpu
from jax.sharding import PartitionSpec as P

entity_rate = 1.0
relation_rate = 0.1

F32 = jnp.float32
BF16 = jnp.bfloat16
MESH = pl.DeviceIdType.MESH


def move(value, offset):
    if offset == 0:
        return value
    regions = lax.axis_size("region")
    count = lax.axis_size("dom")
    z_offset = offset >> 1 & 3
    pairs = []
    for region in range(regions):
        for source in range(count):
            z = source >> 1 & 3
            turn = {0: -1, 3: 1}.get(z, 0) if z_offset > 1 else 0
            target = (region + turn) % regions * count + (source ^ offset)
            pairs.append((region * count + source, target))
    return lax.ppermute(value, ("region", "dom"), pairs)


def route(payload, pattern):
    low = [functools.partial(move, offset=digit) for digit in range(8)]
    high = [functools.partial(move, offset=digit << 3) for digit in range(16)]
    payload = lax.switch(pattern & 7, low, payload)
    return lax.switch(pattern >> 3, high, payload)


def split(value, parts):
    pieces = []
    for _ in range(parts):
        piece = value.astype(BF16)
        pieces.append(piece)
        value = value - piece.astype(F32)
    return pieces


NN = (((1,), (0,)), ((), ()))
NT = (((1,), (1,)), ((), ()))
TN = (((0,), (0,)), ((), ()))


def matmul(pieces, other, dims):
    total = None
    for piece in pieces:
        part = lax.dot_general(piece, other, dims, preferred_element_type=F32)
        total = part if total is None else total + part
    return total


def one_hot(rows, index):
    shape = (rows, index.shape[1])
    return jnp.where(lax.broadcasted_iota(jnp.int32, shape, 0) == index, 1.0, 0.0).astype(BF16)


def terms_kernel(
    count_ref, entity_ref, relation_ref, partner_ref, head_ref, rel_ref, tail_ref, neg_ref,
    head_grad_ref, partner_grad_ref, rel_grad_ref, wide,
):
    features, block = entity_ref.shape
    half = features // 2
    rels = relation_ref.shape[1]
    edges = head_ref.shape[1]
    negatives = neg_ref.shape[0]
    count = count_ref[0]
    head_pick = one_hot(block, head_ref[...])
    rel_pick = one_hot(rels, rel_ref[...])
    tail_pick = one_hot(block, tail_ref[...])
    head = matmul(split(entity_ref[...], 3), head_pick, NN)
    rel = matmul(split(relation_ref[...], 3), rel_pick, NN)
    head_real, head_imag = head[:half], head[half:]
    rel_real, rel_imag = rel[:half], rel[half:]
    wide[:half, :] = head_real * rel_real - head_imag * rel_imag
    wide[half:, :] = head_real * rel_imag + head_imag * rel_real
    query = wide[...].astype(BF16)
    query_wide = query.astype(F32)
    neg_pick = one_hot(block, neg_ref[...].reshape(1, negatives))
    times = lax.dot_general(
        jnp.ones((8, negatives), BF16), neg_pick, NT, preferred_element_type=F32
    )[:1]

    partner = partner_ref[...]
    tail = lax.dot_general(partner, tail_pick, NN, preferred_element_type=F32)
    active = jnp.where(lax.broadcasted_iota(jnp.int32, (1, edges), 1) < count, 1.0, 0.0)
    positive = jnp.sum(query_wide * tail, axis=0, keepdims=True)
    positive_grad = -jax.nn.sigmoid(-positive) * active
    scores = lax.dot_general(query, partner, TN, preferred_element_type=F32)
    share = jnp.where(
        lax.broadcasted_iota(jnp.int32, (edges, 1), 0) < count, 1.0 / negatives, 0.0
    )
    weights = (jax.nn.sigmoid(scores) * share).astype(BF16).astype(F32) * times
    weight_hi, weight_lo = split(weights, 2)
    pull = (
        positive_grad * tail
        + lax.dot_general(partner, weight_hi, NT, preferred_element_type=F32)
        + lax.dot_general(partner, weight_lo, NT, preferred_element_type=F32)
    )
    partner_grad = (
        lax.dot_general(query, weight_hi, NN, preferred_element_type=F32)
        + lax.dot_general(query, weight_lo, NN, preferred_element_type=F32)
        + matmul(split(positive_grad * query_wide, 2), tail_pick, NT)
    )
    partner_grad_ref[...] = partner_grad.astype(BF16)
    pull_real, pull_imag = pull[:half], pull[half:]
    wide[:half, :] = pull_real * head_real + pull_imag * head_imag
    wide[half:, :] = pull_imag * head_real - pull_real * head_imag
    rel_grad_ref[:features, :] = matmul(split(wide[...], 2), rel_pick, NT)
    rel_grad_ref[features:, :] = jnp.zeros((rel_grad_ref.shape[0] - features, rels), F32)
    wide[:half, :] = pull_real * rel_real + pull_imag * rel_imag
    wide[half:, :] = pull_imag * rel_real - pull_real * rel_imag
    head_grad_ref[...] = matmul(split(wide[...], 2), head_pick, NT)


def edge_terms(edge_count, entity, relation, partner, head, rel, tail, neg):
    features, block = entity.shape
    vmem = pl.BlockSpec(memory_space=pltpu.VMEM)
    return pl.pallas_call(
        terms_kernel,
        out_shape=(
            jax.ShapeDtypeStruct((features, block), F32),
            jax.ShapeDtypeStruct((features, block), BF16),
            jax.ShapeDtypeStruct((512, relation.shape[1]), F32),
        ),
        in_specs=[pl.BlockSpec(memory_space=pltpu.SMEM)] + [vmem] * 7,
        out_specs=(vmem, vmem, vmem),
        scratch_shapes=[pltpu.VMEM((features, head.shape[1]), F32)],
        name="edge_terms",
    )(edge_count, entity, relation, partner, head, rel, tail, neg)


def sums_kernel(
    head_ref, returned_ref, rel_ref,
    entity_grad, relation_grad,
    mine, sent, far_up, far_down, both_up, both_down, got, shared,
    core_got, core_sum, x_got, x_sum, y_got, lo_all, pair_mine, pair_got, whole,
    send_sem, recv_sem,
):
    features, block = head_ref.shape
    quarter = block // 4
    region = lax.axis_index("region")
    dom = lax.axis_index("dom")
    x = dom // 32
    y = lax.rem(dom // 8, 4)
    z = lax.rem(dom // 2, 4)
    core = lax.rem(dom, 2)

    def at(region=region, x=x, y=y, z=z, core=core):
        return (region, ((x * 4 + y) * 4 + z) * 2 + core)

    def turn(value, step):
        return lax.rem(value + step, 4)

    def peer(axis, step):
        if axis == "core":
            return at(core=1 - core)
        if axis == "x":
            return at(x=turn(x, step))
        if axis == "y":
            return at(y=turn(y, step))
        if axis == "z":
            return at(z=turn(z, step))
        return at(region=turn(region, step))

    barrier = pltpu.get_barrier_semaphore()
    peers = [peer("core", 1), peer("r", 1), peer("r", 3)]
    peers += [peer(a, s) for a in ("x", "y", "z") for s in (1, 2, 3)]
    for other in peers:
        pl.semaphore_signal(barrier, inc=1, device_id=other, device_id_type=MESH)

    for q in range(4):
        columns = slice(q * quarter, (q + 1) * quarter)
        value = head_ref[:, columns] + returned_ref[:, columns].astype(F32)
        mine[q] = value
        sent[q] = value.astype(BF16)

    pl.semaphore_wait(barrier, len(peers))
    used = [0]

    def send(src, dst, device):
        slot = used[0]
        used[0] += 1
        copy = pltpu.make_async_remote_copy(
            src_ref=src,
            dst_ref=dst,
            send_sem=send_sem.at[slot],
            recv_sem=recv_sem.at[slot],
            device_id=device,
            device_id_type=MESH,
        )
        copy.start()
        return copy

    def wait(copies):
        for copy in copies:
            copy.wait()

    steps = (2, 1, 3)
    up, down, far = turn(region, 1), turn(region, 3), turn(region, 2)
    above, below = peer("r", 1), peer("r", 3)
    first = at(region=region + 1 - 2 * lax.rem(region, 2))
    second = at(region=3 - region)
    cut = far_up.shape[0]
    top, low = pl.ds(0, cut), pl.ds(cut, features - cut)

    far_copies = [
        send(sent.at[far, top], far_up, above),
        send(sent.at[far, low], far_down, below),
    ]
    near_copies = [
        send(sent.at[up, low], got.at[0, low], above),
        send(sent.at[down, top], got.at[1, top], below),
    ]

    wait([send(rel_ref.at[1 - core], core_got, peer("core", 1))])
    core_sum[...] = rel_ref[core] + core_got[...]
    wait([send(core_sum.at[turn(x, s)], x_got.at[s - 1], peer("x", s)) for s in steps])
    x_sum[...] = core_sum[x] + x_got[0] + x_got[1] + x_got[2]
    y_copies = [send(x_sum.at[turn(y, s)], y_got.at[s - 1], peer("y", s)) for s in steps]

    wait(far_copies)
    both_up[...] = (mine[up, :cut] + far_up[...].astype(F32)).astype(BF16)
    both_down[...] = (mine[down, cut:] + far_down[...].astype(F32)).astype(BF16)
    near_copies += [
        send(both_up, got.at[0, top], above),
        send(both_down, got.at[1, low], below),
    ]

    wait(y_copies)
    lo_all[z] = x_sum[y] + y_got[0] + y_got[1] + y_got[2]
    wait([send(lo_all.at[z], lo_all.at[z], peer("z", s)) for s in steps])
    pair_mine[0] = lo_all[0] + lo_all[1] + lo_all[2] + lo_all[3]
    pair_copies = [send(pair_mine.at[0], pair_got.at[0], first)]

    wait(near_copies)
    total = mine[region] + got[0].astype(F32) + got[1].astype(F32)
    shared[region] = total.astype(BF16)
    relayed = [
        send(shared.at[region, top], shared.at[region, top], above),
        send(shared.at[region, low], shared.at[region, low], below),
    ]
    last_copies = [
        send(shared.at[region, low], shared.at[region, low], above),
        send(shared.at[region, top], shared.at[region, top], below),
    ]

    wait(pair_copies)
    pair_mine[1] = pair_mine[0] + pair_got[0]
    pair_copies = [send(pair_mine.at[1], pair_got.at[1], second)]
    wait(relayed)
    last_copies += [
        send(shared.at[down, top], shared.at[down, top], above),
        send(shared.at[up, low], shared.at[up, low], below),
    ]
    wait(pair_copies)
    whole[core, x, y] = pair_mine[1] + pair_got[1]
    wait([send(whole.at[core, x, y], whole.at[core, x, y], peer("y", s)) for s in steps])
    wait([send(whole.at[core, x], whole.at[core, x], peer("x", s)) for s in steps])
    wait([send(whole.at[core], whole.at[core], peer("core", 1))])
    for piece in range(features // 16):
        part = whole[piece // 16, piece // 4 % 4, piece % 4]
        relation_grad[piece * 16 : piece * 16 + 16, :] = part

    wait(last_copies)
    for q in range(4):
        entity_grad[:, q * quarter : (q + 1) * quarter] = shared[q]


def sum_all(head_grad, returned, rel_grad):
    features, block = head_grad.shape
    rels = rel_grad.shape[1]
    quarter = block // 4
    vmem = pl.BlockSpec(memory_space=pltpu.VMEM)
    piece = (16, rels)
    copies = 31
    cut = (features // 2 + 15) // 16 * 16
    return pl.pallas_call(
        sums_kernel,
        out_shape=(
            jax.ShapeDtypeStruct((features, block), BF16),
            jax.ShapeDtypeStruct((features, rels), F32),
        ),
        in_specs=[vmem] * 3,
        out_specs=(vmem, vmem),
        scratch_shapes=[
            pltpu.VMEM((4, features, quarter), F32),
            pltpu.VMEM((4, features, quarter), BF16),
            pltpu.VMEM((cut, quarter), BF16),
            pltpu.VMEM((features - cut, quarter), BF16),
            pltpu.VMEM((cut, quarter), BF16),
            pltpu.VMEM((features - cut, quarter), BF16),
            pltpu.VMEM((2, features, quarter), BF16),
            pltpu.VMEM((4, features, quarter), BF16),
            pltpu.VMEM((4, 4) + piece, F32),
            pltpu.VMEM((4, 4) + piece, F32),
            pltpu.VMEM((3, 4) + piece, F32),
            pltpu.VMEM((4,) + piece, F32),
            pltpu.VMEM((3,) + piece, F32),
            pltpu.VMEM((4,) + piece, F32),
            pltpu.VMEM((2,) + piece, F32),
            pltpu.VMEM((2,) + piece, F32),
            pltpu.VMEM((2, 4, 4) + piece, F32),
            pltpu.SemaphoreType.DMA((copies,)),
            pltpu.SemaphoreType.DMA((copies,)),
        ],
        compiler_params=pltpu.CompilerParams(collective_id=0, has_side_effects=True),
        name="sum_all",
    )(head_grad, returned, rel_grad.reshape((2, 4, 4) + piece))


def shards(
    entity, relation, head_index, relation_index, tail_index, negative_index, plan, edge_count
):
    pattern = plan[0]
    partner = route(entity.astype(BF16), pattern)
    head_grad, partner_grad, rel_grad = edge_terms(
        edge_count,
        entity,
        relation,
        partner,
        head_index[None, :],
        relation_index[None, :],
        tail_index[None, :],
        negative_index,
    )
    returned = route(partner_grad, pattern)
    entity_grad, relation_grad = sum_all(head_grad, returned, rel_grad)
    return entity - entity_rate * entity_grad.astype(F32), relation - relation_rate * relation_grad


def solution(mesh):
    in_specs = (
        P(None, "dom"),
        P(),
        P(("region", "dom")),
        P(("region", "dom")),
        P(("region", "dom")),
        P(("region", "dom")),
        P(),
        P(("region", "dom")),
    )
    out_specs = (P(None, "dom"), P())
    return jax.shard_map(shards, mesh=mesh, in_specs=in_specs, out_specs=out_specs, check_vma=False)
```

```python
import functools

import jax
import jax.numpy as jnp
from jax import lax
from jax.experimental import pallas as pl
from jax.experimental.pallas import tpu as pltpu
from jax.sharding import PartitionSpec as P

entity_rate = 1.0
relation_rate = 0.1

F32 = jnp.float32
BF16 = jnp.bfloat16
MESH = pl.DeviceIdType.MESH


def move(value, offset):
    if offset == 0:
        return value
    regions = lax.axis_size("region")
    count = lax.axis_size("dom")
    z_offset = offset >> 1 & 3
    pairs = []
    for region in range(regions):
        for source in range(count):
            z = source >> 1 & 3
            turn = {0: -1, 3: 1}.get(z, 0) if z_offset > 1 else 0
            target = (region + turn) % regions * count + (source ^ offset)
            pairs.append((region * count + source, target))
    return lax.ppermute(value, ("region", "dom"), pairs)


def route(payload, pattern):
    low = [functools.partial(move, offset=digit) for digit in range(8)]
    high = [functools.partial(move, offset=digit << 3) for digit in range(16)]
    payload = lax.switch(pattern & 7, low, payload)
    return lax.switch(pattern >> 3, high, payload)


def route_beside(payload, rel_grad, pattern):
    def low(digit, value, rel):
        return move(value, digit), scatter_sum(rel)

    def high(digit, value, rel):
        return move(value, digit << 3), along_sum(rel)

    lows = [functools.partial(low, digit) for digit in range(8)]
    highs = [functools.partial(high, digit) for digit in range(16)]
    payload, piece = lax.switch(pattern & 7, lows, payload, rel_grad)
    return lax.switch(pattern >> 3, highs, payload, piece)


def split(value, parts):
    pieces = []
    for _ in range(parts):
        piece = value.astype(BF16)
        pieces.append(piece)
        value = value - piece.astype(F32)
    return pieces


NN = (((1,), (0,)), ((), ()))
NT = (((1,), (1,)), ((), ()))
TN = (((0,), (0,)), ((), ()))


def matmul(pieces, other, dims):
    total = None
    for piece in pieces:
        part = lax.dot_general(piece, other, dims, preferred_element_type=F32)
        total = part if total is None else total + part
    return total


def one_hot(rows, index):
    shape = (rows, index.shape[1])
    return jnp.where(lax.broadcasted_iota(jnp.int32, shape, 0) == index, 1.0, 0.0).astype(BF16)


def terms_kernel(
    count_ref, entity_ref, relation_ref, partner_ref, head_ref, rel_ref, tail_ref, neg_ref,
    head_grad_ref, partner_grad_ref, rel_grad_ref, wide,
):
    features, block = entity_ref.shape
    half = features // 2
    rels = relation_ref.shape[1]
    edges = head_ref.shape[1]
    negatives = neg_ref.shape[0]
    count = count_ref[0]
    head_pick = one_hot(block, head_ref[...])
    rel_pick = one_hot(rels, rel_ref[...])
    tail_pick = one_hot(block, tail_ref[...])
    head = matmul(split(entity_ref[...], 3), head_pick, NN)
    rel = matmul(split(relation_ref[...], 3), rel_pick, NN)
    head_real, head_imag = head[:half], head[half:]
    rel_real, rel_imag = rel[:half], rel[half:]
    wide[:half, :] = head_real * rel_real - head_imag * rel_imag
    wide[half:, :] = head_real * rel_imag + head_imag * rel_real
    query = wide[...].astype(BF16)
    query_wide = query.astype(F32)
    neg_pick = one_hot(block, neg_ref[...].reshape(1, negatives))
    times = lax.dot_general(
        jnp.ones((8, negatives), BF16), neg_pick, NT, preferred_element_type=F32
    )[:1]

    partner = partner_ref[...]
    tail = lax.dot_general(partner, tail_pick, NN, preferred_element_type=F32)
    active = jnp.where(lax.broadcasted_iota(jnp.int32, (1, edges), 1) < count, 1.0, 0.0)
    positive = jnp.sum(query_wide * tail, axis=0, keepdims=True)
    positive_grad = -jax.nn.sigmoid(-positive) * active
    scores = lax.dot_general(query, partner, TN, preferred_element_type=F32)
    share = jnp.where(
        lax.broadcasted_iota(jnp.int32, (edges, 1), 0) < count, 1.0 / negatives, 0.0
    )
    weights = (jax.nn.sigmoid(scores) * share).astype(BF16).astype(F32) * times
    weight_hi, weight_lo = split(weights, 2)
    pull = (
        positive_grad * tail
        + lax.dot_general(partner, weight_hi, NT, preferred_element_type=F32)
        + lax.dot_general(partner, weight_lo, NT, preferred_element_type=F32)
    )
    partner_grad = (
        lax.dot_general(query, weight_hi, NN, preferred_element_type=F32)
        + lax.dot_general(query, weight_lo, NN, preferred_element_type=F32)
        + matmul(split(positive_grad * query_wide, 2), tail_pick, NT)
    )
    partner_grad_ref[...] = partner_grad.astype(BF16)
    pull_real, pull_imag = pull[:half], pull[half:]
    wide[:half, :] = pull_real * head_real + pull_imag * head_imag
    wide[half:, :] = pull_imag * head_real - pull_real * head_imag
    rel_grad_ref[:features, :] = matmul(split(wide[...], 2), rel_pick, NT)
    rel_grad_ref[features:, :] = jnp.zeros((rel_grad_ref.shape[0] - features, rels), F32)
    wide[:half, :] = pull_real * rel_real + pull_imag * rel_imag
    wide[half:, :] = pull_imag * rel_real - pull_real * rel_imag
    head_grad_ref[...] = matmul(split(wide[...], 2), head_pick, NT)


def edge_terms(edge_count, entity, relation, partner, head, rel, tail, neg):
    features, block = entity.shape
    vmem = pl.BlockSpec(memory_space=pltpu.VMEM)
    return pl.pallas_call(
        terms_kernel,
        out_shape=(
            jax.ShapeDtypeStruct((features, block), F32),
            jax.ShapeDtypeStruct((features, block), BF16),
            jax.ShapeDtypeStruct((512, relation.shape[1]), F32),
        ),
        in_specs=[pl.BlockSpec(memory_space=pltpu.SMEM)] + [vmem] * 7,
        out_specs=(vmem, vmem, vmem),
        scratch_shapes=[pltpu.VMEM((features, head.shape[1]), F32)],
        name="edge_terms",
    )(edge_count, entity, relation, partner, head, rel, tail, neg)


def position():
    region = lax.axis_index("region")
    dom = lax.axis_index("dom")
    x = dom // 32
    y = lax.rem(dom // 8, 4)
    z = lax.rem(dom // 2, 4)
    core = lax.rem(dom, 2)

    def at(region=region, x=x, y=y, z=z, core=core):
        return (region, ((x * 4 + y) * 4 + z) * 2 + core)

    def turn(value, step):
        return lax.rem(value + step, 4)

    def peer(axis, step):
        if axis == "core":
            return at(core=1 - core)
        if axis == "x":
            return at(x=turn(x, step))
        if axis == "y":
            return at(y=turn(y, step))
        if axis == "z":
            return at(z=turn(z, step))
        if axis == "pair":
            other = region + 1 - 2 * lax.rem(region, 2) if step == 1 else 3 - region
            return at(region=other)
        return at(region=turn(region, step))

    return region, x, y, z, core, peer, turn


def greet(peers):
    barrier = pltpu.get_barrier_semaphore()
    for other in peers:
        pl.semaphore_signal(barrier, inc=1, device_id=other, device_id_type=MESH)
    return lambda: pl.semaphore_wait(barrier, len(peers))


def sender(send_sem, recv_sem):
    used = [0]

    def send(src, dst, device):
        slot = used[0]
        used[0] += 1
        copy = pltpu.make_async_remote_copy(
            src_ref=src,
            dst_ref=dst,
            send_sem=send_sem.at[slot],
            recv_sem=recv_sem.at[slot],
            device_id=device,
            device_id_type=MESH,
        )
        copy.start()
        return copy

    return send


def wait(copies):
    for copy in copies:
        copy.wait()


def scatter_kernel(
    rel_ref, piece_ref, core_got, core_sum, x_got, x_sum, y_got, send_sem, recv_sem
):
    region, x, y, z, core, peer, turn = position()
    steps = (2, 1, 3)
    greet([peer("core", 1)] + [peer(a, s) for a in ("x", "y") for s in steps])()
    send = sender(send_sem, recv_sem)
    wait([send(rel_ref.at[1 - core], core_got, peer("core", 1))])
    core_sum[...] = rel_ref[core] + core_got[...]
    wait([send(core_sum.at[turn(x, s)], x_got.at[s - 1], peer("x", s)) for s in steps])
    x_sum[...] = core_sum[x] + x_got[0] + x_got[1] + x_got[2]
    wait([send(x_sum.at[turn(y, s)], y_got.at[s - 1], peer("y", s)) for s in steps])
    piece_ref[...] = x_sum[y] + y_got[0] + y_got[1] + y_got[2]


def along_kernel(piece_ref, sum_ref, lo_all, pair_mine, pair_got, send_sem, recv_sem):
    region, x, y, z, core, peer, turn = position()
    steps = (2, 1, 3)
    greet([peer("z", s) for s in steps] + [peer("r", 1), peer("r", 3)])()
    send = sender(send_sem, recv_sem)
    lo_all[z] = piece_ref[...]
    wait([send(lo_all.at[z], lo_all.at[z], peer("z", s)) for s in steps])
    pair_mine[0] = lo_all[0] + lo_all[1] + lo_all[2] + lo_all[3]
    wait([send(pair_mine.at[0], pair_got.at[0], peer("pair", 1))])
    pair_mine[1] = pair_mine[0] + pair_got[0]
    wait([send(pair_mine.at[1], pair_got.at[1], peer("pair", 2))])
    sum_ref[...] = pair_mine[1] + pair_got[1]


def small_sum(kernel, value, scratch, copies, number, name):
    piece = (16, value.shape[-1])
    vmem = pl.BlockSpec(memory_space=pltpu.VMEM)
    return pl.pallas_call(
        kernel,
        out_shape=jax.ShapeDtypeStruct(piece, F32),
        in_specs=[vmem],
        out_specs=vmem,
        scratch_shapes=[pltpu.VMEM(shape + piece, F32) for shape in scratch]
        + [pltpu.SemaphoreType.DMA((copies,))] * 2,
        compiler_params=pltpu.CompilerParams(collective_id=number, has_side_effects=True),
        cost_estimate=pl.CostEstimate(flops=10**7, bytes_accessed=10**7, transcendentals=0),
        name=name,
    )(value)


def scatter_sum(rel_grad):
    value = rel_grad.reshape((2, 4, 4, 16, rel_grad.shape[1]))
    scratch = [(4, 4), (4, 4), (3, 4), (4,), (3,)]
    return small_sum(scatter_kernel, value, scratch, 7, 1, "scatter_sum")


def along_sum(piece):
    return small_sum(along_kernel, piece, [(4,), (2,), (2,)], 5, 2, "along_sum")


def sums_kernel(
    head_ref, returned_ref, rel_ref,
    entity_grad, relation_grad,
    mine, sent, far_up, far_down, both_up, both_down, got, shared,
    whole,
    send_sem, recv_sem,
):
    features, block = head_ref.shape
    quarter = block // 4
    region, x, y, z, core, peer, turn = position()
    peers = [peer("core", 1), peer("r", 1), peer("r", 3)]
    peers += [peer(a, s) for a in ("x", "y") for s in (1, 2, 3)]
    greeted = greet(peers)

    for q in range(4):
        columns = slice(q * quarter, (q + 1) * quarter)
        value = head_ref[:, columns] + returned_ref[:, columns].astype(F32)
        mine[q] = value
        sent[q] = value.astype(BF16)

    greeted()
    send = sender(send_sem, recv_sem)
    steps = (2, 1, 3)
    up, down, far = turn(region, 1), turn(region, 3), turn(region, 2)
    above, below = peer("r", 1), peer("r", 3)
    cut = far_up.shape[0]
    top, low = pl.ds(0, cut), pl.ds(cut, features - cut)

    far_copies = [
        send(sent.at[far, top], far_up, above),
        send(sent.at[far, low], far_down, below),
    ]
    near_copies = [
        send(sent.at[up, low], got.at[0, low], above),
        send(sent.at[down, top], got.at[1, top], below),
    ]

    whole[core, x, y] = rel_ref[...]
    y_copies = [send(whole.at[core, x, y], whole.at[core, x, y], peer("y", s)) for s in steps]

    wait(far_copies)
    both_up[...] = (mine[up, :cut] + far_up[...].astype(F32)).astype(BF16)
    both_down[...] = (mine[down, cut:] + far_down[...].astype(F32)).astype(BF16)
    near_copies += [
        send(both_up, got.at[0, top], above),
        send(both_down, got.at[1, low], below),
    ]

    wait(y_copies)
    x_copies = [send(whole.at[core, x], whole.at[core, x], peer("x", s)) for s in steps]

    wait(near_copies)
    total = mine[region] + got[0].astype(F32) + got[1].astype(F32)
    shared[region] = total.astype(BF16)
    relayed = [
        send(shared.at[region, top], shared.at[region, top], above),
        send(shared.at[region, low], shared.at[region, low], below),
    ]
    last_copies = [
        send(shared.at[region, low], shared.at[region, low], above),
        send(shared.at[region, top], shared.at[region, top], below),
    ]

    wait(x_copies)
    core_copies = [send(whole.at[core], whole.at[core], peer("core", 1))]
    wait(relayed)
    last_copies += [
        send(shared.at[down, top], shared.at[down, top], above),
        send(shared.at[up, low], shared.at[up, low], below),
    ]
    wait(core_copies)
    for piece in range(features // 16):
        part = whole[piece // 16, piece // 4 % 4, piece % 4]
        relation_grad[piece * 16 : piece * 16 + 16, :] = part

    wait(last_copies)
    for q in range(4):
        entity_grad[:, q * quarter : (q + 1) * quarter] = shared[q]


def sum_all(head_grad, returned, rel_piece):
    features, block = head_grad.shape
    rels = rel_piece.shape[1]
    quarter = block // 4
    vmem = pl.BlockSpec(memory_space=pltpu.VMEM)
    piece = (16, rels)
    copies = 19
    cut = (features // 2 + 15) // 16 * 16
    return pl.pallas_call(
        sums_kernel,
        out_shape=(
            jax.ShapeDtypeStruct((features, block), BF16),
            jax.ShapeDtypeStruct((features, rels), F32),
        ),
        in_specs=[vmem] * 3,
        out_specs=(vmem, vmem),
        scratch_shapes=[
            pltpu.VMEM((4, features, quarter), F32),
            pltpu.VMEM((4, features, quarter), BF16),
            pltpu.VMEM((cut, quarter), BF16),
            pltpu.VMEM((features - cut, quarter), BF16),
            pltpu.VMEM((cut, quarter), BF16),
            pltpu.VMEM((features - cut, quarter), BF16),
            pltpu.VMEM((2, features, quarter), BF16),
            pltpu.VMEM((4, features, quarter), BF16),
            pltpu.VMEM((2, 4, 4) + piece, F32),
            pltpu.SemaphoreType.DMA((copies,)),
            pltpu.SemaphoreType.DMA((copies,)),
        ],
        compiler_params=pltpu.CompilerParams(collective_id=0, has_side_effects=True),
        name="sum_all",
    )(head_grad, returned, rel_piece)


def shards(
    entity, relation, head_index, relation_index, tail_index, negative_index, plan, edge_count
):
    pattern = plan[0]
    partner = route(entity.astype(BF16), pattern)
    head_grad, partner_grad, rel_grad = edge_terms(
        edge_count,
        entity,
        relation,
        partner,
        head_index[None, :],
        relation_index[None, :],
        tail_index[None, :],
        negative_index,
    )
    returned, rel_piece = route_beside(partner_grad, rel_grad, pattern)
    entity_grad, relation_grad = sum_all(head_grad, returned, rel_piece)
    return entity - entity_rate * entity_grad.astype(F32), relation - relation_rate * relation_grad


def solution(mesh):
    in_specs = (
        P(None, "dom"),
        P(),
        P(("region", "dom")),
        P(("region", "dom")),
        P(("region", "dom")),
        P(("region", "dom")),
        P(),
        P(("region", "dom")),
    )
    out_specs = (P(None, "dom"), P())
    return jax.shard_map(shards, mesh=mesh, in_specs=in_specs, out_specs=out_specs, check_vma=False)
```

```python
import functools

import jax
import jax.numpy as jnp
from jax import lax
from jax.experimental import pallas as pl
from jax.experimental.pallas import tpu as pltpu
from jax.sharding import PartitionSpec as P

entity_rate = 1.0
relation_rate = 0.1

F32 = jnp.float32
BF16 = jnp.bfloat16
MESH = pl.DeviceIdType.MESH


def move(value, offset):
    if offset == 0:
        return value
    regions = lax.axis_size("region")
    count = lax.axis_size("dom")
    z_offset = offset >> 1 & 3
    pairs = []
    for region in range(regions):
        for source in range(count):
            z = source >> 1 & 3
            turn = {0: -1, 3: 1}.get(z, 0) if z_offset > 1 else 0
            target = (region + turn) % regions * count + (source ^ offset)
            pairs.append((region * count + source, target))
    return lax.ppermute(value, ("region", "dom"), pairs)


def route(payload, pattern):
    low = [functools.partial(move, offset=digit) for digit in range(8)]
    high = [functools.partial(move, offset=digit << 3) for digit in range(16)]
    payload = lax.switch(pattern & 7, low, payload)
    return lax.switch(pattern >> 3, high, payload)


def route_beside(payload, rel_grad, pattern):
    def low(digit, value, rel):
        return move(value, digit), scatter_sum(rel)

    def high(digit, value, rel):
        return move(value, digit << 3), along_sum(rel)

    lows = [functools.partial(low, digit) for digit in range(8)]
    highs = [functools.partial(high, digit) for digit in range(16)]
    payload, piece = lax.switch(pattern & 7, lows, payload, rel_grad)
    return lax.switch(pattern >> 3, highs, payload, piece)


def split(value, parts):
    pieces = []
    for _ in range(parts):
        piece = value.astype(BF16)
        pieces.append(piece)
        value = value - piece.astype(F32)
    return pieces


NN = (((1,), (0,)), ((), ()))
NT = (((1,), (1,)), ((), ()))
TN = (((0,), (0,)), ((), ()))


def matmul(pieces, other, dims):
    total = None
    for piece in pieces:
        part = lax.dot_general(piece, other, dims, preferred_element_type=F32)
        total = part if total is None else total + part
    return total


def one_hot(rows, index):
    shape = (rows, index.shape[1])
    return jnp.where(lax.broadcasted_iota(jnp.int32, shape, 0) == index, 1.0, 0.0).astype(BF16)


def terms_kernel(
    count_ref, entity_ref, relation_ref, partner_ref, head_ref, rel_ref, tail_ref, neg_ref,
    head_grad_ref, partner_grad_ref, rel_grad_ref, wide,
):
    features, block = entity_ref.shape
    half = features // 2
    rels = relation_ref.shape[1]
    edges = head_ref.shape[1]
    negatives = neg_ref.shape[0]
    count = count_ref[0]
    head_pick = one_hot(block, head_ref[...])
    rel_pick = one_hot(rels, rel_ref[...])
    tail_pick = one_hot(block, tail_ref[...])
    head = matmul(split(entity_ref[...], 3), head_pick, NN)
    rel = matmul(split(relation_ref[...], 3), rel_pick, NN)
    head_real, head_imag = head[:half], head[half:]
    rel_real, rel_imag = rel[:half], rel[half:]
    wide[:half, :] = head_real * rel_real - head_imag * rel_imag
    wide[half:, :] = head_real * rel_imag + head_imag * rel_real
    query = wide[...].astype(BF16)
    query_wide = query.astype(F32)
    neg_pick = one_hot(block, neg_ref[...].reshape(1, negatives))
    times = lax.dot_general(
        jnp.ones((8, negatives), BF16), neg_pick, NT, preferred_element_type=F32
    )[:1]

    partner = partner_ref[...]
    tail = lax.dot_general(partner, tail_pick, NN, preferred_element_type=F32)
    active = jnp.where(lax.broadcasted_iota(jnp.int32, (1, edges), 1) < count, 1.0, 0.0)
    positive = jnp.sum(query_wide * tail, axis=0, keepdims=True)
    positive_grad = -jax.nn.sigmoid(-positive) * active
    scores = lax.dot_general(query, partner, TN, preferred_element_type=F32)
    share = jnp.where(
        lax.broadcasted_iota(jnp.int32, (edges, 1), 0) < count, 1.0 / negatives, 0.0
    )
    weights = (jax.nn.sigmoid(scores) * share).astype(BF16).astype(F32) * times
    weight_hi, weight_lo = split(weights, 2)
    pull = (
        positive_grad * tail
        + lax.dot_general(partner, weight_hi, NT, preferred_element_type=F32)
        + lax.dot_general(partner, weight_lo, NT, preferred_element_type=F32)
    )
    partner_grad = (
        lax.dot_general(query, weight_hi, NN, preferred_element_type=F32)
        + lax.dot_general(query, weight_lo, NN, preferred_element_type=F32)
        + matmul(split(positive_grad * query_wide, 2), tail_pick, NT)
    )
    partner_grad_ref[...] = partner_grad.astype(BF16)
    pull_real, pull_imag = pull[:half], pull[half:]
    wide[:half, :] = pull_real * head_real + pull_imag * head_imag
    wide[half:, :] = pull_imag * head_real - pull_real * head_imag
    rel_grad_ref[:features, :] = matmul(split(wide[...], 2), rel_pick, NT)
    rel_grad_ref[features:, :] = jnp.zeros((rel_grad_ref.shape[0] - features, rels), F32)
    wide[:half, :] = pull_real * rel_real + pull_imag * rel_imag
    wide[half:, :] = pull_imag * rel_real - pull_real * rel_imag
    head_grad_ref[...] = matmul(split(wide[...], 2), head_pick, NT)


def edge_terms(edge_count, entity, relation, partner, head, rel, tail, neg):
    features, block = entity.shape
    vmem = pl.BlockSpec(memory_space=pltpu.VMEM)
    return pl.pallas_call(
        terms_kernel,
        out_shape=(
            jax.ShapeDtypeStruct((features, block), F32),
            jax.ShapeDtypeStruct((features, block), BF16),
            jax.ShapeDtypeStruct((512, relation.shape[1]), F32),
        ),
        in_specs=[pl.BlockSpec(memory_space=pltpu.SMEM)] + [vmem] * 7,
        out_specs=(vmem, vmem, vmem),
        scratch_shapes=[pltpu.VMEM((features, head.shape[1]), F32)],
        name="edge_terms",
    )(edge_count, entity, relation, partner, head, rel, tail, neg)


def position():
    region = lax.axis_index("region")
    dom = lax.axis_index("dom")
    x = dom // 32
    y = lax.rem(dom // 8, 4)
    z = lax.rem(dom // 2, 4)
    core = lax.rem(dom, 2)

    def at(region=region, x=x, y=y, z=z, core=core):
        return (region, ((x * 4 + y) * 4 + z) * 2 + core)

    def turn(value, step):
        return lax.rem(value + step, 4)

    def peer(axis, step):
        if axis == "core":
            return at(core=1 - core)
        if axis == "x":
            return at(x=turn(x, step))
        if axis == "y":
            return at(y=turn(y, step))
        if axis == "z":
            return at(z=turn(z, step))
        if axis == "pair":
            other = region + 1 - 2 * lax.rem(region, 2) if step == 1 else 3 - region
            return at(region=other)
        return at(region=turn(region, step))

    return region, x, y, z, core, peer, turn


def greet(peers):
    barrier = pltpu.get_barrier_semaphore()
    for other in peers:
        pl.semaphore_signal(barrier, inc=1, device_id=other, device_id_type=MESH)
    return lambda: pl.semaphore_wait(barrier, len(peers))


def sender(send_sem, recv_sem):
    used = [0]

    def send(src, dst, device):
        slot = used[0]
        used[0] += 1
        copy = pltpu.make_async_remote_copy(
            src_ref=src,
            dst_ref=dst,
            send_sem=send_sem.at[slot],
            recv_sem=recv_sem.at[slot],
            device_id=device,
            device_id_type=MESH,
        )
        copy.start()
        return copy

    return send


def wait(copies):
    for copy in copies:
        copy.wait()


def scatter_kernel(
    rel_ref, piece_ref, core_got, core_sum, x_got, x_sum, y_got, send_sem, recv_sem
):
    region, x, y, z, core, peer, turn = position()
    steps = (2, 1, 3)
    greet([peer("core", 1)] + [peer(a, s) for a in ("x", "y") for s in steps])()
    send = sender(send_sem, recv_sem)
    wait([send(rel_ref.at[1 - core], core_got, peer("core", 1))])
    core_sum[...] = rel_ref[core] + core_got[...]
    wait([send(core_sum.at[turn(x, s)], x_got.at[s - 1], peer("x", s)) for s in steps])
    x_sum[...] = core_sum[x] + x_got[0] + x_got[1] + x_got[2]
    wait([send(x_sum.at[turn(y, s)], y_got.at[s - 1], peer("y", s)) for s in steps])
    piece_ref[...] = x_sum[y] + y_got[0] + y_got[1] + y_got[2]


def along_kernel(piece_ref, sum_ref, lo_all, send_sem, recv_sem):
    region, x, y, z, core, peer, turn = position()
    steps = (2, 1, 3)
    greet([peer("z", s) for s in steps])()
    send = sender(send_sem, recv_sem)
    lo_all[z] = piece_ref[...]
    wait([send(lo_all.at[z], lo_all.at[z], peer("z", s)) for s in steps])
    sum_ref[...] = lo_all[0] + lo_all[1] + lo_all[2] + lo_all[3]


def small_sum(kernel, value, scratch, copies, number, name):
    piece = (16, value.shape[-1])
    vmem = pl.BlockSpec(memory_space=pltpu.VMEM)
    return pl.pallas_call(
        kernel,
        out_shape=jax.ShapeDtypeStruct(piece, F32),
        in_specs=[vmem],
        out_specs=vmem,
        scratch_shapes=[pltpu.VMEM(shape + piece, F32) for shape in scratch]
        + [pltpu.SemaphoreType.DMA((copies,))] * 2,
        compiler_params=pltpu.CompilerParams(collective_id=number, has_side_effects=True),
        cost_estimate=pl.CostEstimate(flops=10**7, bytes_accessed=10**7, transcendentals=0),
        name=name,
    )(value)


def scatter_sum(rel_grad):
    value = rel_grad.reshape((2, 4, 4, 16, rel_grad.shape[1]))
    scratch = [(4, 4), (4, 4), (3, 4), (4,), (3,)]
    return small_sum(scatter_kernel, value, scratch, 7, 1, "scatter_sum")


def along_sum(piece):
    return small_sum(along_kernel, piece, [(4,)], 3, 2, "along_sum")


def sums_kernel(
    head_ref, returned_ref, rel_ref,
    entity_grad, relation_grad,
    mine, sent, far_up, far_down, both_up, both_down, got, shared,
    pair_mine, pair_got, whole,
    send_sem, recv_sem,
):
    features, block = head_ref.shape
    quarter = block // 4
    region, x, y, z, core, peer, turn = position()
    peers = [peer("core", 1), peer("r", 1), peer("r", 3)]
    peers += [peer(a, s) for a in ("x", "y") for s in (1, 2, 3)]
    greeted = greet(peers)

    for q in range(4):
        columns = slice(q * quarter, (q + 1) * quarter)
        value = head_ref[:, columns] + returned_ref[:, columns].astype(F32)
        mine[q] = value
        sent[q] = value.astype(BF16)

    greeted()
    send = sender(send_sem, recv_sem)
    steps = (2, 1, 3)
    up, down, far = turn(region, 1), turn(region, 3), turn(region, 2)
    above, below = peer("r", 1), peer("r", 3)
    cut = far_up.shape[0]
    top, low = pl.ds(0, cut), pl.ds(cut, features - cut)

    pair_mine[0] = rel_ref[...]
    pair_copies = [send(pair_mine.at[0], pair_got.at[0], peer("pair", 1))]
    far_copies = [
        send(sent.at[far, top], far_up, above),
        send(sent.at[far, low], far_down, below),
    ]
    near_copies = [
        send(sent.at[up, low], got.at[0, low], above),
        send(sent.at[down, top], got.at[1, top], below),
    ]

    wait(pair_copies)
    pair_mine[1] = pair_mine[0] + pair_got[0]
    pair_copies = [send(pair_mine.at[1], pair_got.at[1], peer("pair", 2))]

    wait(far_copies)
    both_up[...] = (mine[up, :cut] + far_up[...].astype(F32)).astype(BF16)
    both_down[...] = (mine[down, cut:] + far_down[...].astype(F32)).astype(BF16)
    near_copies += [
        send(both_up, got.at[0, top], above),
        send(both_down, got.at[1, low], below),
    ]

    wait(pair_copies)
    whole[core, x, y] = pair_mine[1] + pair_got[1]
    y_copies = [send(whole.at[core, x, y], whole.at[core, x, y], peer("y", s)) for s in steps]

    wait(near_copies)
    total = mine[region] + got[0].astype(F32) + got[1].astype(F32)
    shared[region] = total.astype(BF16)
    relayed = [
        send(shared.at[region, top], shared.at[region, top], above),
        send(shared.at[region, low], shared.at[region, low], below),
    ]
    last_copies = [
        send(shared.at[region, low], shared.at[region, low], above),
        send(shared.at[region, top], shared.at[region, top], below),
    ]
    wait(y_copies)
    x_copies = [send(whole.at[core, x], whole.at[core, x], peer("x", s)) for s in steps]

    wait(x_copies)
    core_copies = [send(whole.at[core], whole.at[core], peer("core", 1))]
    wait(relayed)
    last_copies += [
        send(shared.at[down, top], shared.at[down, top], above),
        send(shared.at[up, low], shared.at[up, low], below),
    ]
    wait(core_copies)
    for piece in range(features // 16):
        part = whole[piece // 16, piece // 4 % 4, piece % 4]
        relation_grad[piece * 16 : piece * 16 + 16, :] = part

    wait(last_copies)
    for q in range(4):
        entity_grad[:, q * quarter : (q + 1) * quarter] = shared[q]


def sum_all(head_grad, returned, rel_piece):
    features, block = head_grad.shape
    rels = rel_piece.shape[1]
    quarter = block // 4
    vmem = pl.BlockSpec(memory_space=pltpu.VMEM)
    piece = (16, rels)
    copies = 21
    cut = (features // 2 + 15) // 16 * 16
    return pl.pallas_call(
        sums_kernel,
        out_shape=(
            jax.ShapeDtypeStruct((features, block), BF16),
            jax.ShapeDtypeStruct((features, rels), F32),
        ),
        in_specs=[vmem] * 3,
        out_specs=(vmem, vmem),
        scratch_shapes=[
            pltpu.VMEM((4, features, quarter), F32),
            pltpu.VMEM((4, features, quarter), BF16),
            pltpu.VMEM((cut, quarter), BF16),
            pltpu.VMEM((features - cut, quarter), BF16),
            pltpu.VMEM((cut, quarter), BF16),
            pltpu.VMEM((features - cut, quarter), BF16),
            pltpu.VMEM((2, features, quarter), BF16),
            pltpu.VMEM((4, features, quarter), BF16),
            pltpu.VMEM((2,) + piece, F32),
            pltpu.VMEM((2,) + piece, F32),
            pltpu.VMEM((2, 4, 4) + piece, F32),
            pltpu.SemaphoreType.DMA((copies,)),
            pltpu.SemaphoreType.DMA((copies,)),
        ],
        compiler_params=pltpu.CompilerParams(collective_id=0, has_side_effects=True),
        name="sum_all",
    )(head_grad, returned, rel_piece)


def shards(
    entity, relation, head_index, relation_index, tail_index, negative_index, plan, edge_count
):
    pattern = plan[0]
    partner = route(entity.astype(BF16), pattern)
    head_grad, partner_grad, rel_grad = edge_terms(
        edge_count,
        entity,
        relation,
        partner,
        head_index[None, :],
        relation_index[None, :],
        tail_index[None, :],
        negative_index,
    )
    returned, rel_piece = route_beside(partner_grad, rel_grad, pattern)
    entity_grad, relation_grad = sum_all(head_grad, returned, rel_piece)
    return entity - entity_rate * entity_grad.astype(F32), relation - relation_rate * relation_grad


def solution(mesh):
    in_specs = (
        P(None, "dom"),
        P(),
        P(("region", "dom")),
        P(("region", "dom")),
        P(("region", "dom")),
        P(("region", "dom")),
        P(),
        P(("region", "dom")),
    )
    out_specs = (P(None, "dom"), P())
    return jax.shard_map(shards, mesh=mesh, in_specs=in_specs, out_specs=out_specs, check_vma=False)
```
